32 devices in a mesh: dp: 4 (over x, core), ctx: 8 (over z, y).
Axes of the slice: x: 2, y: 2, z: 4, core: 2. Of those that a mesh axis runs over, the one named last changes fastest.
Arguments:
- projections: bfloat16 [4, 3, 2048, 1024], P('dp', None, None, 'ctx'), may hold values from -6 to 6
- short_filter: float32 [3, 2048, 3], replicated, may hold values from -3.5 to 3.5
- long_filter: float32 [2048, 1024], P(None, 'ctx'), may hold values from -0.1875 to 0.1875
- skip_gain: float32 [2048], replicated, may hold values from -4 to 4
- cotangent: bfloat16 [4, 2048, 1024], P('dp', None, 'ctx'), may hold values from -6 to 6
Outputs:
- layer_out: bfloat16 [4, 2048, 1024], P('dp', None, 'ctx')
- proj_grad: bfloat16 [4, 3, 2048, 1024], P('dp', None, None, 'ctx')
- filter_grad: float32 [2048, 1024], P('dp', 'ctx')
The draws below stay inside these ranges and needn't reach their ends.
All inputs are finite; a program needn't handle non-finite values.
Results may differ from the reference program's by a relative error of at most 0.0049.
Values may be sent and summed in bfloat16 or wider, within the bound.
No kernel may reach another device: no remote copies, remote signals or barrier semaphores. Data moves between devices by JAX's collectives and lax.ppermute only.
A program may use at most 128 MiB of HBM per device.

```python
import math
import jax
import jax.numpy as jnp
from jax import lax

C = 2048
LENGTH = 1024
SEQS = 4


def block_scale(key, dims, split, least, high):
    loudness, own = 1.0, jax.random.fold_in(key, 6)
    for axis_at, parts in split:
        draws = jnp.exp(jax.random.uniform(jax.random.fold_in(own, axis_at), (parts,), jnp.float32, least / len(split), high / len(split)))
        loudness = loudness * jnp.repeat(draws, dims[axis_at] // parts).reshape([-1 if axis == axis_at else 1 for axis in range(len(dims))])
    return loudness


def normal_values(rng, extent, scale, reach, pieces=(), dtype=jnp.bfloat16):
    entries = scale * jax.random.normal(rng, extent, jnp.float32)
    if pieces:
        entries = entries * block_scale(rng, extent, pieces, -0.22, 0.18)
    return jnp.clip(entries, -reach, reach).astype(dtype)


def setup_inputs(seed: int = 0) -> dict:
    key_of = jax.random.split(jax.random.key(seed), 6)
    projections = normal_values(key_of[0], (SEQS, 3, C, LENGTH), 1.0, 6.0, ((0, 4), (3, 8)))
    short_filter = normal_values(key_of[1], (3, C, 3), 3 ** -0.5, 3.5, (), jnp.float32)
    long_filter = normal_values(key_of[2], (C, LENGTH), LENGTH ** -0.5, 0.1875, ((1, 8),), jnp.float32)
    skip_gain = normal_values(key_of[3], (C,), 1.0, 4.0, (), jnp.float32)
    cotangent = normal_values(key_of[4], (SEQS, C, LENGTH), 1.0, 6.0, ((0, 4), (2, 8)))
    return {"projections": projections, "short_filter": short_filter, "long_filter": long_filter, "skip_gain": skip_gain, "cotangent": cotangent}


def delayed(values, steps):
    padded = jnp.pad(values, ((0, 0), (0, 0), (steps, 0)))
    return padded[:, :, :LENGTH]

def advanced(values, steps):
    padded = jnp.pad(values, ((0, 0), (0, 0), (0, steps)))
    return padded[:, :, steps:]

def reference(projections, short_filter, long_filter, skip_gain, cotangent):
    fft_size = 2 * LENGTH
    filter_spec = jnp.fft.rfft(long_filter, n=fft_size, axis=-1)
    tap_zero = short_filter[:, :, 0:1]
    tap_one = short_filter[:, :, 1:2]
    tap_two = short_filter[:, :, 2:3]
    skip_col = skip_gain[:, None]
    scale = 1.0 / math.sqrt(SEQS * LENGTH)
    outs_list = []
    grads_list = []
    filter_total = jnp.zeros((C, LENGTH), jnp.float32)
    for index in range(SEQS):
        inputs = projections[index].astype(jnp.float32)
        act = tap_zero * inputs + tap_one * delayed(inputs, 1) + tap_two * delayed(inputs, 2)
        first = act[0]
        second = act[1]
        value = act[2]
        gate = lax.optimization_barrier((first * value).astype(jnp.bfloat16)).astype(jnp.float32)
        gate_spec = jnp.fft.rfft(gate, n=fft_size, axis=-1)
        conv = jnp.fft.irfft(filter_spec * gate_spec, n=fft_size, axis=-1)[:, :LENGTH]
        mixed = conv + skip_col * gate
        outs_list.append((second * mixed).astype(jnp.bfloat16))
        upstream = cotangent[index].astype(jnp.float32)
        grad = lax.optimization_barrier((upstream * second).astype(jnp.bfloat16)).astype(jnp.float32)
        grad_spec = jnp.fft.rfft(grad, n=fft_size, axis=-1)
        corr = jnp.fft.irfft(jnp.conj(filter_spec) * grad_spec, n=fft_size, axis=-1)[:, :LENGTH]
        filter_total = filter_total + jnp.fft.irfft(jnp.conj(gate_spec) * grad_spec, n=fft_size, axis=-1)[:, :LENGTH]
        gate_grad = corr + skip_col * grad
        act_grad = jnp.stack([gate_grad * value, upstream * mixed, gate_grad * first])
        proj_back = tap_zero * act_grad + tap_one * advanced(act_grad, 1) + tap_two * advanced(act_grad, 2)
        grads_list.append(proj_back.astype(jnp.bfloat16))
    return (jnp.stack(outs_list), jnp.stack(grads_list), filter_total * scale)
```

```python
import functools
import math

import jax
import jax.numpy as jnp
import numpy as np
from jax import lax
from jax.experimental import pallas as pl
from jax.experimental.pallas import tpu as pltpu
from jax.sharding import PartitionSpec as P

exact_mode = lax.Precision.HIGHEST
f32 = jnp.float32
bf16 = jnp.bfloat16
TABLE_BYTES = 16 * 2**20


def angle_table(rows, cols, period):
    row_index = lax.broadcasted_iota(jnp.int32, (rows, cols), 0)
    col_index = lax.broadcasted_iota(jnp.int32, (rows, cols), 1)
    product = row_index * col_index % period
    return product.astype(jnp.float32) * (2.0 * math.pi / period)


def forward_dft(signal):
    groups = signal.shape[0]
    blocks = signal.shape[1]
    inner = signal.shape[3]
    outer = 2 * blocks
    total = outer * inner
    first_angle = angle_table(outer, blocks, outer)
    first_cos = jnp.broadcast_to(jnp.cos(first_angle), (groups, outer, blocks))
    first_sin = jnp.broadcast_to(-jnp.sin(first_angle), (groups, outer, blocks))
    part_real = jnp.einsum("dqp,dpsr->dqsr", first_cos, signal, precision=exact_mode)
    part_imag = jnp.einsum("dqp,dpsr->dqsr", first_sin, signal, precision=exact_mode)
    twist = angle_table(outer, inner, total)
    twist_cos = jnp.cos(twist)[None, :, None, :]
    twist_sin = jnp.sin(twist)[None, :, None, :]
    mid_real = part_real * twist_cos + part_imag * twist_sin
    mid_imag = part_imag * twist_cos - part_real * twist_sin
    last_angle = angle_table(inner, inner, inner)
    last_cos = jnp.cos(last_angle)
    last_sin = jnp.sin(last_angle)
    out_real = jnp.einsum("dqsr,rm->dqsm", mid_real, last_cos, precision=exact_mode) + jnp.einsum(
        "dqsr,rm->dqsm", mid_imag, last_sin, precision=exact_mode
    )
    out_imag = jnp.einsum("dqsr,rm->dqsm", mid_imag, last_cos, precision=exact_mode) - jnp.einsum(
        "dqsr,rm->dqsm", mid_real, last_sin, precision=exact_mode
    )
    return (out_real, out_imag)


def inverse_dft(spectrum):
    spec_real, spec_imag = spectrum
    groups = spec_real.shape[0]
    outer = spec_real.shape[1]
    inner = spec_real.shape[3]
    blocks = outer // 2
    total = outer * inner
    last_angle = angle_table(inner, inner, inner)
    last_cos = jnp.cos(last_angle)
    last_sin = jnp.sin(last_angle)
    mid_real = jnp.einsum("dqsm,mr->dqsr", spec_real, last_cos, precision=exact_mode) - jnp.einsum(
        "dqsm,mr->dqsr", spec_imag, last_sin, precision=exact_mode
    )
    mid_imag = jnp.einsum("dqsm,mr->dqsr", spec_real, last_sin, precision=exact_mode) + jnp.einsum(
        "dqsm,mr->dqsr", spec_imag, last_cos, precision=exact_mode
    )
    twist = angle_table(outer, inner, total)
    twist_cos = jnp.cos(twist)[None, :, None, :]
    twist_sin = jnp.sin(twist)[None, :, None, :]
    turned_real = mid_real * twist_cos - mid_imag * twist_sin
    turned_imag = mid_real * twist_sin + mid_imag * twist_cos
    first_angle = angle_table(blocks, outer, outer)
    first_cos = jnp.broadcast_to(jnp.cos(first_angle), (groups, blocks, outer))
    first_sin = jnp.broadcast_to(jnp.sin(first_angle), (groups, blocks, outer))
    result = jnp.einsum(
        "dpq,dqsr->dpsr", first_cos, turned_real, precision=exact_mode
    ) - jnp.einsum("dpq,dqsr->dpsr", first_sin, turned_imag, precision=exact_mode)
    return result * (1.0 / total)


def spec_product(left, right):
    return (left[0] * right[0] - left[1] * right[1], left[0] * right[1] + left[1] * right[0])


def conj_product(left, right):
    return (left[0] * right[0] + left[1] * right[1], left[0] * right[1] - left[1] * right[0])


def whole(shape):
    return pl.BlockSpec(shape, lambda k: (0,) * len(shape))


def cost(flops, nbytes):
    return pl.CostEstimate(flops=int(flops), bytes_accessed=int(nbytes), transcendentals=0)


def pick(rows, cols, pairs):
    r = lax.broadcasted_iota(jnp.int32, (rows, cols), 0)
    c = lax.broadcasted_iota(jnp.int32, (rows, cols), 1)
    hit = functools.reduce(jnp.logical_or, [(r == a) & (c == b) for a, b in pairs])
    return jnp.where(hit, 1.0, 0.0).astype(bf16)


def nt(a, b):
    return lax.dot_general(a, b, (((1,), (1,)), ((), ())), preferred_element_type=f32)


def tn(a, b):
    return lax.dot_general(a, b, (((0,), (0,)), ((), ())), preferred_element_type=f32)


def flat(value, rows):
    return value.astype(f32).reshape(rows, value.shape[-1])


def edge_kernel(rows, inner, proj_ref, cot_ref, filt_ref, last_ref, first_ref, filt_out):
    last = jnp.zeros((8, rows), f32)
    first = jnp.zeros((8, rows), f32)
    for m in range(4):
        source = proj_ref[m] if m < 3 else cot_ref[...]
        value = flat(source, rows).astype(bf16)
        if m < 3:
            last += nt(pick(8, inner, [(2 * m, inner - 2), (2 * m + 1, inner - 1)]), value)
        first += nt(pick(8, inner, [(2 * m, 0), (2 * m + 1, 1)]), value)
    last_ref[0] = last.astype(bf16)
    first_ref[0] = first.astype(bf16)
    filt_out[0] = flat(filt_ref[...], rows).astype(bf16)


def activations(rows, inner, proj_ref, prev, taps):
    spots = []
    for m in range(3):
        at = 2 * inner * m
        spots += [(2 * m + 1, at), (2 * m, at + inner), (2 * m + 1, at + inner + 1)]
    placed = tn(prev, pick(8, 6 * inner, spots))
    lane = lax.broadcasted_iota(jnp.int32, (rows, inner), 1)
    act = []
    for m in range(3):
        x = flat(proj_ref[m], rows)
        one = placed[:, 2 * inner * m : 2 * inner * m + inner]
        two = placed[:, 2 * inner * m + inner : 2 * inner * (m + 1)]
        x1 = jnp.where(lane < 1, one, pltpu.roll(x, 1, 1))
        x2 = jnp.where(lane < 2, two, pltpu.roll(x, 2, 1))
        act.append(taps[m][:, 0:1] * x + taps[m][:, 1:2] * x1 + taps[m][:, 2:3] * x2)
    return act


def gate_kernel(rows, inner, proj_ref, cot_ref, prev_ref, taps_ref, gate_ref, grad_ref):
    taps = [flat(taps_ref[m], rows) for m in range(3)]
    first, second, value = activations(rows, inner, proj_ref, prev_ref[0], taps)
    gate_ref[0] = (first * value).astype(bf16)
    grad_ref[0] = (flat(cot_ref[...], rows) * second).astype(bf16)


def split(value):
    high = value.astype(bf16)
    low = (value - high.astype(f32)).astype(bf16)
    return jnp.concatenate([high, low], axis=0)


ROOT_HALF = math.sqrt(0.5)


def spectrum(x_ref, small_ref, large_ref, spec_ref):
    n, rows, inner = x_ref.shape
    per = n // 4
    q = per * inner
    x0, x1, x2, x3 = (
        jnp.concatenate([x_ref[p * per + i].astype(f32) for i in range(per)], axis=1) for p in range(4)
    )

    def put(at, value, table):
        both = jnp.dot(split(value), table, preferred_element_type=f32)
        spec_ref[:, at * q : at * q + table.shape[1]] = both[:rows] + both[rows:]

    even, odd = x0 + x2, x1 + x3
    put(0, even + odd, small_ref[0])
    put(1, even - odd, small_ref[1])
    put(4, jnp.concatenate([x0 - x2, x3 - x1], axis=1), large_ref[1])
    turn_a, turn_b = (x1 - x3) * ROOT_HALF, odd * ROOT_HALF
    put(2, jnp.concatenate([x0 + turn_a, -x2 - turn_b], axis=1), large_ref[0])
    put(6, jnp.concatenate([x0 - turn_a, x2 - turn_b], axis=1), large_ref[2])


def product_inverse(a_ref, b_ref, conj, small_ref, large_ref, q):
    rows = a_ref.shape[0]

    def back(at, width, table):
        half = width // 2
        start = at * q
        ar, ai = a_ref[:, start : start + half], a_ref[:, start + half : start + width]
        br, bi = b_ref[:, start : start + half], b_ref[:, start + half : start + width]
        rr, ii, ri, ir = ar * br, ai * bi, ar * bi, ai * br
        re, im = (rr + ii, ri - ir) if conj else (rr - ii, ri + ir)
        if at == 0:
            lane = lax.broadcasted_iota(jnp.int32, (rows, half), 1)
            re = jnp.where(lane == 0, 0.5 * rr, re)
            im = jnp.where(lane == 0, 0.5 * ii, im)
        scale = 2.0 / (8 * q)
        both = jnp.concatenate([re * scale, im * scale], axis=1).astype(bf16)
        return nt(both, table)

    v0 = back(0, q, small_ref[0])
    v4 = back(1, q, small_ref[1])
    u2 = back(4, 2 * q, large_ref[1])
    r2, i2 = u2[:, :q], u2[:, q:]
    e0, e1, e2, e3 = v0 + v4 + r2, v0 - v4 - i2, v0 + v4 - r2, v0 - v4 + i2
    u1 = back(2, 2 * q, large_ref[0])
    u3 = back(6, 2 * q, large_ref[2])
    r1, i1, r3, i3 = u1[:, :q], u1[:, q:], u3[:, :q], u3[:, q:]
    o1 = (r1 - i1 - r3 - i3) * ROOT_HALF
    o3 = (r3 - i3 - r1 - i1) * ROOT_HALF
    return e0 + r1 + r3, e1 + o1, e2 - i1 + i3, e3 + o3


def blocks_of(quarters, inner):
    per = quarters[0].shape[1] // inner
    return [part[:, i * inner : (i + 1) * inner] for part in quarters for i in range(per)]


def store_result(out_ref, blocks, rows, inner):
    lanes = -(-rows // 128) * 128
    rounded = [b.astype(bf16) for b in blocks]
    for k, block in enumerate(rounded):
        out_ref[k, :rows] = block
        if k + 1 < len(rounded):
            after = rounded[k + 1]
            if lanes > rows:
                after = jnp.concatenate([after, jnp.zeros((lanes - rows, inner), bf16)], axis=0)
            tail = nt(pick(8, inner, [(0, 0), (1, 1)]), after)
        else:
            tail = jnp.zeros((8, lanes), f32)
        parts = [tail[:, i : i + 128] for i in range(0, lanes, 128)]
        out_ref[k, rows : rows + 8 * len(parts)] = jnp.concatenate(parts, axis=0).astype(bf16)


def filter_kernel(filt_ref, small_ref, large_ref, spec_ref):
    spectrum(filt_ref, small_ref, large_ref, spec_ref)


def conv_kernel(gate_ref, filt_spec, small_ref, large_ref, gate_spec, out_ref):
    n, rows, inner = gate_ref.shape
    spectrum(gate_ref, small_ref, large_ref, gate_spec)
    parts = product_inverse(filt_spec, gate_spec, False, small_ref, large_ref, n * inner // 4)
    store_result(out_ref, blocks_of(parts, inner), rows, inner)


def fgrad_kernel(grad_ref, gate_spec, small_ref, large_ref, grad_spec, out_ref):
    n, rows, inner = grad_ref.shape
    spectrum(grad_ref, small_ref, large_ref, grad_spec)
    parts = product_inverse(gate_spec, grad_spec, True, small_ref, large_ref, n * inner // 4)
    groups, _, slab, _ = out_ref.shape
    for k, block in enumerate(blocks_of(parts, inner)):
        for d in range(groups):
            out_ref[d, k] = block[d * slab : (d + 1) * slab].astype(out_ref.dtype)


def corr_kernel(grad_spec, filt_spec, small_ref, large_ref, own_ref, got_ref, out_ref):
    n, slab, inner = own_ref.shape
    rows = grad_spec.shape[0]
    parts = product_inverse(filt_spec, grad_spec, True, small_ref, large_ref, n * inner // 4)
    store_result(out_ref, blocks_of(parts, inner), rows, inner)
    at = out_ref.shape[1] - slab
    for k in range(n):
        total = own_ref[k].astype(f32)
        for e in range(got_ref.shape[0]):
            total = total + got_ref[e, k].astype(f32)
        out_ref[k, at:] = total.astype(bf16)


def result_kernel(
    rows,
    inner,
    scale,
    proj_ref,
    cot_ref,
    prev_ref,
    own_ref,
    next_ref,
    taps_ref,
    skip_ref,
    row_ref,
    conv_ref,
    corr_ref,
    out_ref,
    pg_ref,
    fg_ref,
):
    taps = [flat(taps_ref[m], rows) for m in range(3)]
    skip = flat(skip_ref[...], rows)
    first, second, value = activations(rows, inner, proj_ref, prev_ref[0], taps)
    upstream = flat(cot_ref[...], rows)
    gate = (first * value).astype(bf16).astype(f32)
    grad = (upstream * second).astype(bf16).astype(f32)
    mixed = conv_ref[0, :rows].astype(f32) + skip * gate
    out_ref[...] = (second * mixed).astype(bf16).reshape(out_ref.shape)
    gate_grad = corr_ref[0, :rows].astype(f32) + skip * grad
    act_grad = (gate_grad * value, upstream * mixed, gate_grad * first)

    lanes = -(-rows // 128) * 128

    def tail_of(ref):
        parts = [ref[0, rows + 8 * i : rows + 8 * i + 8].astype(f32) for i in range(lanes // 128)]
        return jnp.concatenate(parts, axis=1)[:, :rows]

    conv_tail, corr_tail = tail_of(conv_ref), tail_of(corr_ref)
    own = own_ref[0].astype(f32)
    after = next_ref[0].astype(f32)
    param = row_ref[0]
    spare = []
    for t in range(2):
        ahead = []
        for m in range(3):
            history = (after[2 * m + t : 2 * m + t + 1],) + (
                (own[2 * m + 1 : 2 * m + 2], own[2 * m : 2 * m + 1])
                if t == 0
                else (after[2 * m : 2 * m + 1], own[2 * m + 1 : 2 * m + 2])
            )
            ahead.append(
                param[3 * m : 3 * m + 1] * history[0]
                + param[3 * m + 1 : 3 * m + 2] * history[1]
                + param[3 * m + 2 : 3 * m + 3] * history[2]
            )
        above = after[6 + t : 7 + t]
        keep = param[9:10]
        gate_t = (ahead[0] * ahead[2]).astype(bf16).astype(f32)
        grad_t = (above * ahead[1]).astype(bf16).astype(f32)
        mixed_t = conv_tail[t : t + 1] + keep * gate_t
        gate_grad_t = corr_tail[t : t + 1] + keep * grad_t
        spare.append((gate_grad_t * ahead[2], above * mixed_t, gate_grad_t * ahead[0]))
    line = lax.broadcasted_iota(jnp.int32, (8, rows), 0)
    beyond = jnp.zeros((8, rows), f32)
    for m in range(3):
        for t in range(2):
            beyond = jnp.where(line == 2 * m + t, spare[t][m], beyond)
    high = beyond.astype(bf16)
    low = (beyond - high.astype(f32)).astype(bf16)
    spots = []
    for m in range(3):
        at = 2 * inner * m
        spots += [(2 * m, at + inner - 1), (2 * m, at + 2 * inner - 2), (2 * m + 1, at + 2 * inner - 1)]
    where_to = pick(8, 6 * inner, spots)
    placed = tn(high, where_to) + tn(low, where_to)
    lane = lax.broadcasted_iota(jnp.int32, (rows, inner), 1)
    for m in range(3):
        x = act_grad[m]
        one = placed[:, 2 * inner * m : 2 * inner * m + inner]
        two = placed[:, 2 * inner * m + inner : 2 * inner * (m + 1)]
        x1 = jnp.where(lane >= inner - 1, one, pltpu.roll(x, inner - 1, 1))
        x2 = jnp.where(lane >= inner - 2, two, pltpu.roll(x, inner - 2, 1))
        back = taps[m][:, 0:1] * x + taps[m][:, 1:2] * x1 + taps[m][:, 2:3] * x2
        pg_ref[m] = back.astype(bf16).reshape(pg_ref.shape[1:])
    slab = fg_ref.shape[1]
    fg_ref[0] = corr_ref[0, corr_ref.shape[1] - slab :].astype(f32) * scale


def dft_tables(q):
    r = np.arange(q)[:, None]
    step = 2.0 * np.pi / (8 * q)

    def angle(residue, count):
        return (r * (residue + 8 * np.arange(count)[None, :]) % (8 * q)) * step

    small = []
    for residue in (0, 4):
        a = angle(residue, q // 2)
        table = np.concatenate([np.cos(a), -np.sin(a)], axis=1)
        if residue == 0:
            table[:, q // 2] = 1.0 - 2.0 * (np.arange(q) % 2)
        small.append(table)
    large = []
    for residue in (1, 2, 3):
        a = angle(residue, q)
        large.append(np.block([[np.cos(a), -np.sin(a)], [np.sin(a), np.cos(a)]]))
    return (np.stack(small).astype(jnp.bfloat16), np.stack(large).astype(jnp.bfloat16))


def shards(projections, short_filter, long_filter, skip_gain, cotangent):
    groups = lax.axis_size("dp")
    n = lax.axis_size("ctx")
    channels = projections.shape[2]
    inner = projections.shape[3]
    slab = channels // (groups * n)
    rows = groups * slab
    length = inner * n
    q = length // 4
    tail_rows = 8 * -(-rows // 128)

    proj = projections.reshape(3, groups, n, slab, inner)
    cot = cotangent.reshape(groups, n, slab, inner)
    filt = long_filter.reshape(groups, n, slab, inner)
    taps = short_filter.reshape(3, groups, n, slab, 3)
    skip = skip_gain.reshape(groups, n, slab, 1)
    row_taps = jnp.transpose(taps, (2, 0, 4, 1, 3)).reshape(n, 9, rows)
    row_skip = jnp.transpose(skip, (1, 3, 0, 2)).reshape(n, 1, rows)
    row_param = jnp.concatenate([row_taps, row_skip, jnp.zeros((n, 6, rows), f32)], axis=1)

    proj_spec = pl.BlockSpec((3, groups, None, slab, inner), lambda k: (0, 0, k, 0, 0))
    cot_spec = pl.BlockSpec((groups, None, slab, inner), lambda k: (0, k, 0, 0))
    taps_spec = pl.BlockSpec((3, groups, None, slab, 3), lambda k: (0, 0, k, 0, 0))
    skip_spec = pl.BlockSpec((groups, None, slab, 1), lambda k: (0, k, 0, 0))
    edge_spec = pl.BlockSpec((1, 8, rows), lambda k: (k, 0, 0))
    row_spec = pl.BlockSpec((1, 16, rows), lambda k: (k, 0, 0))

    def block_spec(count):
        return pl.BlockSpec((1, count, inner), lambda k: (k, 0, 0))

    def block_shape(count):
        return jax.ShapeDtypeStruct((n, count, inner), bf16)

    edge_shape = jax.ShapeDtypeStruct((n, 8, rows), bf16)
    size = channels * inner

    last, first, filt_rows = pl.pallas_call(
        functools.partial(edge_kernel, rows, inner),
        grid=(n,),
        in_specs=[proj_spec, cot_spec, cot_spec],
        out_specs=[edge_spec, edge_spec, block_spec(rows)],
        out_shape=[edge_shape, edge_shape, block_shape(rows)],
        cost_estimate=cost(64 * size, 14 * size),
        name="edges",
    )(proj, cot, filt)
    forth = [(i, i + 1) for i in range(n - 1)]
    prev = lax.ppermute(last, "ctx", forth)
    after = lax.ppermute(first, "ctx", [(b, a) for a, b in forth])

    gate, grad = pl.pallas_call(
        functools.partial(gate_kernel, rows, inner),
        grid=(n,),
        in_specs=[proj_spec, cot_spec, edge_spec, taps_spec],
        out_specs=[block_spec(rows), block_spec(rows)],
        out_shape=[block_shape(rows), block_shape(rows)],
        cost_estimate=cost(2000 * size, 16 * size),
        name="gates",
    )(proj, cot, prev, taps)

    def across(value):
        return lax.all_to_all(value, "ctx", split_axis=0, concat_axis=0, tiled=True)

    filt_ch = across(filt_rows)
    gate_ch = across(gate)
    grad_ch = across(grad)

    me = lax.axis_index("dp")
    scale = 1.0 / math.sqrt(groups * length)

    def from_others(pieces):
        got = []
        for e in range(1, groups):
            piece = lax.dynamic_index_in_dim(pieces, lax.rem(me + e, groups), 0, keepdims=False)
            got.append(lax.ppermute(piece, "dp", [(i, (i + e) % groups) for i in range(groups)]))
        return lax.dynamic_index_in_dim(pieces, me, 0, keepdims=False), jnp.stack(got)

    if n % 4 == 0 and 2 * (14 * q * q) <= TABLE_BYTES:
        small, large = (jnp.asarray(t) for t in dft_tables(q))
        spec_shape = jax.ShapeDtypeStruct((rows, 8 * q), f32)
        dft = 2 * rows * 14 * q * q

        def call(kernel, outs, factor, name, *args):
            return pl.pallas_call(
                kernel,
                out_shape=outs,
                cost_estimate=cost(factor * dft, 30 * rows * q * 4),
                name=name,
            )(*args)

        filt_spec = call(filter_kernel, spec_shape, 2, "filter_spectrum", filt_ch, small, large)
        gate_spec, conv_send = call(
            conv_kernel, [spec_shape, block_shape(rows + tail_rows)], 3, "conv", gate_ch, filt_spec, small, large
        )
        conv_pos = across(conv_send)
        grad_spec, pieces = call(
            fgrad_kernel,
            [spec_shape, jax.ShapeDtypeStruct((groups, n, slab, inner), bf16)],
            3,
            "filter_gradient",
            grad_ch,
            gate_spec,
            small,
            large,
        )
        own, got = from_others(pieces)
        corr_send = call(
            corr_kernel,
            block_shape(rows + tail_rows + slab),
            1,
            "corr",
            grad_spec,
            filt_spec,
            small,
            large,
            own,
            got,
        )
        corr_pos = across(corr_send)
    else:

        def grouped(value):
            return jnp.transpose(value.reshape(n, groups, slab, inner), (1, 0, 2, 3)).astype(f32)

        filt_spec = forward_dft(grouped(filt_ch))
        gate_spec = forward_dft(grouped(gate_ch))
        grad_spec = forward_dft(grouped(grad_ch))

        def returned(spec):
            value = jnp.transpose(inverse_dft(spec), (1, 0, 2, 3)).reshape(n, rows, inner).astype(bf16)
            tail = jnp.transpose(value[1:, :, 0:2], (0, 2, 1))
            lanes = 16 * tail_rows
            tail = jnp.pad(tail, ((0, 1), (0, 6), (0, lanes - rows)))
            tail = jnp.transpose(tail.reshape(n, 8, lanes // 128, 128), (0, 2, 1, 3)).reshape(n, tail_rows, 128)
            return jnp.concatenate([value, tail], axis=1)

        own, got = from_others(inverse_dft(conj_product(gate_spec, grad_spec)).astype(bf16))
        total = (own.astype(f32) + jnp.sum(got.astype(f32), axis=0)).astype(bf16)
        conv_pos = across(returned(spec_product(filt_spec, gate_spec)))
        corr_pos = across(jnp.concatenate([returned(conj_product(filt_spec, grad_spec)), total], axis=1))

    layer_out, proj_grad, filter_grad = pl.pallas_call(
        functools.partial(result_kernel, rows, inner, scale),
        grid=(n,),
        in_specs=[
            proj_spec,
            cot_spec,
            edge_spec,
            edge_spec,
            edge_spec,
            taps_spec,
            skip_spec,
            row_spec,
            block_spec(rows + tail_rows),
            block_spec(rows + tail_rows + slab),
        ],
        out_specs=[cot_spec, proj_spec, pl.BlockSpec((1, slab, inner), lambda k: (k, 0, 0))],
        out_shape=[
            jax.ShapeDtypeStruct(cot.shape, bf16),
            jax.ShapeDtypeStruct(proj.shape, bf16),
            jax.ShapeDtypeStruct((n, slab, inner), f32),
        ],
        cost_estimate=cost(2000 * size, 24 * size),
        name="results",
    )(proj, cot, prev, last, after, taps, skip, row_param, conv_pos, corr_pos)
    return (
        layer_out.reshape(1, channels, inner),
        proj_grad.reshape(1, 3, channels, inner),
        filter_grad.reshape(n * slab, inner),
    )


def solution(mesh):
    placed = (P("dp", None, None, "ctx"), P(), P(None, "ctx"), P(), P("dp", None, "ctx"))
    return jax.shard_map(
        shards,
        mesh=mesh,
        in_specs=placed,
        out_specs=(P("dp", None, "ctx"), P("dp", None, None, "ctx"), P("dp", "ctx")),
        check_vma=False,
    )
```

```python
import functools
import math

import jax
import jax.numpy as jnp
import numpy as np
from jax import lax
from jax.experimental import pallas as pl
from jax.experimental.pallas import tpu as pltpu
from jax.sharding import PartitionSpec as P


exact_mode = lax.Precision.HIGHEST
f32 = jnp.float32
bf16 = jnp.bfloat16
TABLE_BYTES = 16 * 2**20


def angle_table(rows, cols, period):
    row_index = lax.broadcasted_iota(jnp.int32, (rows, cols), 0)
    col_index = lax.broadcasted_iota(jnp.int32, (rows, cols), 1)
    product = row_index * col_index % period
    return product.astype(jnp.float32) * (2.0 * math.pi / period)


def forward_dft(signal):
    groups = signal.shape[0]
    blocks = signal.shape[1]
    inner = signal.shape[3]
    outer = 2 * blocks
    total = outer * inner
    first_angle = angle_table(outer, blocks, outer)
    first_cos = jnp.broadcast_to(jnp.cos(first_angle), (groups, outer, blocks))
    first_sin = jnp.broadcast_to(-jnp.sin(first_angle), (groups, outer, blocks))
    part_real = jnp.einsum("dqp,dpsr->dqsr", first_cos, signal, precision=exact_mode)
    part_imag = jnp.einsum("dqp,dpsr->dqsr", first_sin, signal, precision=exact_mode)
    twist = angle_table(outer, inner, total)
    twist_cos = jnp.cos(twist)[None, :, None, :]
    twist_sin = jnp.sin(twist)[None, :, None, :]
    mid_real = part_real * twist_cos + part_imag * twist_sin
    mid_imag = part_imag * twist_cos - part_real * twist_sin
    last_angle = angle_table(inner, inner, inner)
    last_cos = jnp.cos(last_angle)
    last_sin = jnp.sin(last_angle)
    out_real = jnp.einsum("dqsr,rm->dqsm", mid_real, last_cos, precision=exact_mode) + jnp.einsum(
        "dqsr,rm->dqsm", mid_imag, last_sin, precision=exact_mode
    )
    out_imag = jnp.einsum("dqsr,rm->dqsm", mid_imag, last_cos, precision=exact_mode) - jnp.einsum(
        "dqsr,rm->dqsm", mid_real, last_sin, precision=exact_mode
    )
    return (out_real, out_imag)


def inverse_dft(spectrum):
    spec_real, spec_imag = spectrum
    groups = spec_real.shape[0]
    outer = spec_real.shape[1]
    inner = spec_real.shape[3]
    blocks = outer // 2
    total = outer * inner
    last_angle = angle_table(inner, inner, inner)
    last_cos = jnp.cos(last_angle)
    last_sin = jnp.sin(last_angle)
    mid_real = jnp.einsum("dqsm,mr->dqsr", spec_real, last_cos, precision=exact_mode) - jnp.einsum(
        "dqsm,mr->dqsr", spec_imag, last_sin, precision=exact_mode
    )
    mid_imag = jnp.einsum("dqsm,mr->dqsr", spec_real, last_sin, precision=exact_mode) + jnp.einsum(
        "dqsm,mr->dqsr", spec_imag, last_cos, precision=exact_mode
    )
    twist = angle_table(outer, inner, total)
    twist_cos = jnp.cos(twist)[None, :, None, :]
    twist_sin = jnp.sin(twist)[None, :, None, :]
    turned_real = mid_real * twist_cos - mid_imag * twist_sin
    turned_imag = mid_real * twist_sin + mid_imag * twist_cos
    first_angle = angle_table(blocks, outer, outer)
    first_cos = jnp.broadcast_to(jnp.cos(first_angle), (groups, blocks, outer))
    first_sin = jnp.broadcast_to(jnp.sin(first_angle), (groups, blocks, outer))
    result = jnp.einsum(
        "dpq,dqsr->dpsr", first_cos, turned_real, precision=exact_mode
    ) - jnp.einsum("dpq,dqsr->dpsr", first_sin, turned_imag, precision=exact_mode)
    return result * (1.0 / total)


def spec_product(left, right):
    return (left[0] * right[0] - left[1] * right[1], left[0] * right[1] + left[1] * right[0])


def conj_product(left, right):
    return (left[0] * right[0] + left[1] * right[1], left[0] * right[1] - left[1] * right[0])


def cost(flops, nbytes):
    return pl.CostEstimate(flops=int(flops), bytes_accessed=int(nbytes), transcendentals=0)


def pick(rows, cols, pairs):
    r = lax.broadcasted_iota(jnp.int32, (rows, cols), 0)
    c = lax.broadcasted_iota(jnp.int32, (rows, cols), 1)
    hit = functools.reduce(jnp.logical_or, [(r == a) & (c == b) for a, b in pairs])
    return jnp.where(hit, 1.0, 0.0).astype(bf16)


def nt(a, b):
    return lax.dot_general(a, b, (((1,), (1,)), ((), ())), preferred_element_type=f32)


def tn(a, b):
    return lax.dot_general(a, b, (((0,), (0,)), ((), ())), preferred_element_type=f32)


def flat(value, rows):
    return value.astype(f32).reshape(rows, value.shape[-1])


def edge_kernel(rows, inner, proj_ref, cot_ref, filt_ref, last_ref, first_ref, filt_out):
    last = jnp.zeros((8, rows), f32)
    first = jnp.zeros((8, rows), f32)
    for m in range(4):
        source = proj_ref[m] if m < 3 else cot_ref[...]
        value = flat(source, rows).astype(bf16)
        if m < 3:
            last += nt(pick(8, inner, [(2 * m, inner - 2), (2 * m + 1, inner - 1)]), value)
        first += nt(pick(8, inner, [(2 * m, 0), (2 * m + 1, 1)]), value)
    last_ref[0] = last.astype(bf16)
    first_ref[0] = first.astype(bf16)
    filt_out[0] = flat(filt_ref[...], rows).astype(bf16)


def activations(rows, inner, proj_ref, prev, taps):
    spots = []
    for m in range(3):
        at = 2 * inner * m
        spots += [(2 * m + 1, at), (2 * m, at + inner), (2 * m + 1, at + inner + 1)]
    placed = tn(prev, pick(8, 6 * inner, spots))
    lane = lax.broadcasted_iota(jnp.int32, (rows, inner), 1)
    act = []
    for m in range(3):
        x = flat(proj_ref[m], rows)
        one = placed[:, 2 * inner * m : 2 * inner * m + inner]
        two = placed[:, 2 * inner * m + inner : 2 * inner * (m + 1)]
        x1 = jnp.where(lane < 1, one, pltpu.roll(x, 1, 1))
        x2 = jnp.where(lane < 2, two, pltpu.roll(x, 2, 1))
        act.append(taps[m][:, 0:1] * x + taps[m][:, 1:2] * x1 + taps[m][:, 2:3] * x2)
    return act


def block_gate_kernel(rows, inner, proj_ref, cot_ref, prev_ref, taps_ref, gate_ref, grad_ref):
    taps = [flat(taps_ref[m], rows) for m in range(3)]
    first, second, value = activations(rows, inner, proj_ref, prev_ref[0], taps)
    gate_ref[0] = (first * value).astype(bf16)
    grad_ref[0] = (flat(cot_ref[...], rows) * second).astype(bf16)


def split(value):
    high = value.astype(bf16)
    low = (value - high.astype(f32)).astype(bf16)
    return jnp.concatenate([high, low], axis=0)


ROOT_HALF = math.sqrt(0.5)


def spectrum(x_ref, small_ref, large_ref, spec_ref):
    n, rows, inner = x_ref.shape
    per = n // 4
    q = per * inner
    x0, x1, x2, x3 = (
        jnp.concatenate([x_ref[p * per + i].astype(f32) for i in range(per)], axis=1) for p in range(4)
    )

    def put(at, value, table):
        both = jnp.dot(split(value), table, preferred_element_type=f32)
        spec_ref[:, at * q : at * q + table.shape[1]] = both[:rows] + both[rows:]

    even, odd = x0 + x2, x1 + x3
    put(0, even + odd, small_ref[0])
    put(1, even - odd, small_ref[1])
    put(4, jnp.concatenate([x0 - x2, x3 - x1], axis=1), large_ref[1])
    turn_a, turn_b = (x1 - x3) * ROOT_HALF, odd * ROOT_HALF
    put(2, jnp.concatenate([x0 + turn_a, -x2 - turn_b], axis=1), large_ref[0])
    put(6, jnp.concatenate([x0 - turn_a, x2 - turn_b], axis=1), large_ref[2])


def product_inverse(a_ref, b_ref, conj, small_ref, large_ref, q):
    rows = a_ref.shape[0]

    def back(at, width, table):
        half = width // 2
        start = at * q
        ar, ai = a_ref[:, start : start + half], a_ref[:, start + half : start + width]
        br, bi = b_ref[:, start : start + half], b_ref[:, start + half : start + width]
        rr, ii, ri, ir = ar * br, ai * bi, ar * bi, ai * br
        re, im = (rr + ii, ri - ir) if conj else (rr - ii, ri + ir)
        if at == 0:
            lane = lax.broadcasted_iota(jnp.int32, (rows, half), 1)
            re = jnp.where(lane == 0, 0.5 * rr, re)
            im = jnp.where(lane == 0, 0.5 * ii, im)
        scale = 2.0 / (8 * q)
        both = jnp.concatenate([re * scale, im * scale], axis=1).astype(bf16)
        return nt(both, table)

    v0 = back(0, q, small_ref[0])
    v4 = back(1, q, small_ref[1])
    u2 = back(4, 2 * q, large_ref[1])
    r2, i2 = u2[:, :q], u2[:, q:]
    e0, e1, e2, e3 = v0 + v4 + r2, v0 - v4 - i2, v0 + v4 - r2, v0 - v4 + i2
    u1 = back(2, 2 * q, large_ref[0])
    u3 = back(6, 2 * q, large_ref[2])
    r1, i1, r3, i3 = u1[:, :q], u1[:, q:], u3[:, :q], u3[:, q:]
    o1 = (r1 - i1 - r3 - i3) * ROOT_HALF
    o3 = (r3 - i3 - r1 - i1) * ROOT_HALF
    return e0 + r1 + r3, e1 + o1, e2 - i1 + i3, e3 + o3


def blocks_of(quarters, inner):
    per = quarters[0].shape[1] // inner
    return [part[:, i * inner : (i + 1) * inner] for part in quarters for i in range(per)]


def result_kernel(
    rows,
    inner,
    scale,
    proj_ref,
    cot_ref,
    prev_ref,
    own_ref,
    next_ref,
    taps_ref,
    skip_ref,
    row_ref,
    conv_ref,
    corr_ref,
    out_ref,
    pg_ref,
    fg_ref,
):
    taps = [flat(taps_ref[m], rows) for m in range(3)]
    skip = flat(skip_ref[...], rows)
    first, second, value = activations(rows, inner, proj_ref, prev_ref[0], taps)
    upstream = flat(cot_ref[...], rows)
    gate = (first * value).astype(bf16).astype(f32)
    grad = (upstream * second).astype(bf16).astype(f32)
    mixed = conv_ref[0, :rows].astype(f32) + skip * gate
    out_ref[...] = (second * mixed).astype(bf16).reshape(out_ref.shape)
    gate_grad = corr_ref[0, :rows].astype(f32) + skip * grad
    act_grad = (gate_grad * value, upstream * mixed, gate_grad * first)

    lanes = -(-rows // 128) * 128

    def tail_of(ref):
        parts = [ref[0, rows + 8 * i : rows + 8 * i + 8].astype(f32) for i in range(lanes // 128)]
        return jnp.concatenate(parts, axis=1)[:, :rows]

    conv_tail, corr_tail = tail_of(conv_ref), tail_of(corr_ref)
    own = own_ref[0].astype(f32)
    after = next_ref[0].astype(f32)
    param = row_ref[0]
    spare = []
    for t in range(2):
        ahead = []
        for m in range(3):
            history = (after[2 * m + t : 2 * m + t + 1],) + (
                (own[2 * m + 1 : 2 * m + 2], own[2 * m : 2 * m + 1])
                if t == 0
                else (after[2 * m : 2 * m + 1], own[2 * m + 1 : 2 * m + 2])
            )
            ahead.append(
                param[3 * m : 3 * m + 1] * history[0]
                + param[3 * m + 1 : 3 * m + 2] * history[1]
                + param[3 * m + 2 : 3 * m + 3] * history[2]
            )
        above = after[6 + t : 7 + t]
        keep = param[9:10]
        gate_t = (ahead[0] * ahead[2]).astype(bf16).astype(f32)
        grad_t = (above * ahead[1]).astype(bf16).astype(f32)
        mixed_t = conv_tail[t : t + 1] + keep * gate_t
        gate_grad_t = corr_tail[t : t + 1] + keep * grad_t
        spare.append((gate_grad_t * ahead[2], above * mixed_t, gate_grad_t * ahead[0]))
    line = lax.broadcasted_iota(jnp.int32, (8, rows), 0)
    beyond = jnp.zeros((8, rows), f32)
    for m in range(3):
        for t in range(2):
            beyond = jnp.where(line == 2 * m + t, spare[t][m], beyond)
    high = beyond.astype(bf16)
    low = (beyond - high.astype(f32)).astype(bf16)
    spots = []
    for m in range(3):
        at = 2 * inner * m
        spots += [(2 * m, at + inner - 1), (2 * m, at + 2 * inner - 2), (2 * m + 1, at + 2 * inner - 1)]
    where_to = pick(8, 6 * inner, spots)
    placed = tn(high, where_to) + tn(low, where_to)
    lane = lax.broadcasted_iota(jnp.int32, (rows, inner), 1)
    for m in range(3):
        x = act_grad[m]
        one = placed[:, 2 * inner * m : 2 * inner * m + inner]
        two = placed[:, 2 * inner * m + inner : 2 * inner * (m + 1)]
        x1 = jnp.where(lane >= inner - 1, one, pltpu.roll(x, inner - 1, 1))
        x2 = jnp.where(lane >= inner - 2, two, pltpu.roll(x, inner - 2, 1))
        back = taps[m][:, 0:1] * x + taps[m][:, 1:2] * x1 + taps[m][:, 2:3] * x2
        pg_ref[m] = back.astype(bf16).reshape(pg_ref.shape[1:])
    slab = fg_ref.shape[1]
    fg_ref[0] = corr_ref[0, corr_ref.shape[1] - slab :].astype(f32) * scale


def dft_tables(q):
    r = np.arange(q)[:, None]
    step = 2.0 * np.pi / (8 * q)

    def angle(residue, count):
        return (r * (residue + 8 * np.arange(count)[None, :]) % (8 * q)) * step

    small = []
    for residue in (0, 4):
        a = angle(residue, q // 2)
        table = np.concatenate([np.cos(a), -np.sin(a)], axis=1)
        if residue == 0:
            table[:, q // 2] = 1.0 - 2.0 * (np.arange(q) % 2)
        small.append(table)
    large = []
    for residue in (1, 2, 3):
        a = angle(residue, q)
        large.append(np.block([[np.cos(a), -np.sin(a)], [np.sin(a), np.cos(a)]]))
    return (np.stack(small).astype(jnp.bfloat16), np.stack(large).astype(jnp.bfloat16))


def wide_shards(projections, short_filter, long_filter, skip_gain, cotangent):
    groups = lax.axis_size("dp")
    n = lax.axis_size("ctx")
    channels = projections.shape[2]
    inner = projections.shape[3]
    slab = channels // (groups * n)
    rows = groups * slab
    length = inner * n
    tail_rows = 8 * -(-rows // 128)

    proj = projections.reshape(3, groups, n, slab, inner)
    cot = cotangent.reshape(groups, n, slab, inner)
    filt = long_filter.reshape(groups, n, slab, inner)
    taps = short_filter.reshape(3, groups, n, slab, 3)
    skip = skip_gain.reshape(groups, n, slab, 1)
    row_taps = jnp.transpose(taps, (2, 0, 4, 1, 3)).reshape(n, 9, rows)
    row_skip = jnp.transpose(skip, (1, 3, 0, 2)).reshape(n, 1, rows)
    row_param = jnp.concatenate([row_taps, row_skip, jnp.zeros((n, 6, rows), f32)], axis=1)

    proj_spec = pl.BlockSpec((3, groups, None, slab, inner), lambda k: (0, 0, k, 0, 0))
    cot_spec = pl.BlockSpec((groups, None, slab, inner), lambda k: (0, k, 0, 0))
    taps_spec = pl.BlockSpec((3, groups, None, slab, 3), lambda k: (0, 0, k, 0, 0))
    skip_spec = pl.BlockSpec((groups, None, slab, 1), lambda k: (0, k, 0, 0))
    edge_spec = pl.BlockSpec((1, 8, rows), lambda k: (k, 0, 0))
    row_spec = pl.BlockSpec((1, 16, rows), lambda k: (k, 0, 0))

    def block_spec(count):
        return pl.BlockSpec((1, count, inner), lambda k: (k, 0, 0))

    def block_shape(count):
        return jax.ShapeDtypeStruct((n, count, inner), bf16)

    edge_shape = jax.ShapeDtypeStruct((n, 8, rows), bf16)
    size = channels * inner

    last, first, filt_rows = pl.pallas_call(
        functools.partial(edge_kernel, rows, inner),
        grid=(n,),
        in_specs=[proj_spec, cot_spec, cot_spec],
        out_specs=[edge_spec, edge_spec, block_spec(rows)],
        out_shape=[edge_shape, edge_shape, block_shape(rows)],
        cost_estimate=cost(64 * size, 14 * size),
        name="edges",
    )(proj, cot, filt)
    forth = [(i, i + 1) for i in range(n - 1)]
    prev = lax.ppermute(last, "ctx", forth)
    after = lax.ppermute(first, "ctx", [(b, a) for a, b in forth])

    gate, grad = pl.pallas_call(
        functools.partial(block_gate_kernel, rows, inner),
        grid=(n,),
        in_specs=[proj_spec, cot_spec, edge_spec, taps_spec],
        out_specs=[block_spec(rows), block_spec(rows)],
        out_shape=[block_shape(rows), block_shape(rows)],
        cost_estimate=cost(2000 * size, 16 * size),
        name="gates",
    )(proj, cot, prev, taps)

    def across(value):
        return lax.all_to_all(value, "ctx", split_axis=0, concat_axis=0, tiled=True)

    filt_ch = across(filt_rows)
    gate_ch = across(gate)
    grad_ch = across(grad)

    me = lax.axis_index("dp")
    scale = 1.0 / math.sqrt(groups * length)

    def from_others(pieces):
        got = []
        for e in range(1, groups):
            piece = lax.dynamic_index_in_dim(pieces, lax.rem(me + e, groups), 0, keepdims=False)
            got.append(lax.ppermute(piece, "dp", [(i, (i + e) % groups) for i in range(groups)]))
        return lax.dynamic_index_in_dim(pieces, me, 0, keepdims=False), jnp.stack(got)

    def grouped(value):
        return jnp.transpose(value.reshape(n, groups, slab, inner), (1, 0, 2, 3)).astype(f32)

    filt_spec = forward_dft(grouped(filt_ch))
    gate_spec = forward_dft(grouped(gate_ch))
    grad_spec = forward_dft(grouped(grad_ch))

    def returned(spec):
        value = jnp.transpose(inverse_dft(spec), (1, 0, 2, 3)).reshape(n, rows, inner).astype(bf16)
        tail = jnp.transpose(value[1:, :, 0:2], (0, 2, 1))
        lanes = 16 * tail_rows
        tail = jnp.pad(tail, ((0, 1), (0, 6), (0, lanes - rows)))
        tail = jnp.transpose(tail.reshape(n, 8, lanes // 128, 128), (0, 2, 1, 3)).reshape(n, tail_rows, 128)
        return jnp.concatenate([value, tail], axis=1)

    own, got = from_others(inverse_dft(conj_product(gate_spec, grad_spec)).astype(bf16))
    total = (own.astype(f32) + jnp.sum(got.astype(f32), axis=0)).astype(bf16)
    conv_pos = across(returned(spec_product(filt_spec, gate_spec)))
    corr_pos = across(jnp.concatenate([returned(conj_product(filt_spec, grad_spec)), total], axis=1))

    layer_out, proj_grad, filter_grad = pl.pallas_call(
        functools.partial(result_kernel, rows, inner, scale),
        grid=(n,),
        in_specs=[
            proj_spec,
            cot_spec,
            edge_spec,
            edge_spec,
            edge_spec,
            taps_spec,
            skip_spec,
            row_spec,
            block_spec(rows + tail_rows),
            block_spec(rows + tail_rows + slab),
        ],
        out_specs=[cot_spec, proj_spec, pl.BlockSpec((1, slab, inner), lambda k: (k, 0, 0))],
        out_shape=[
            jax.ShapeDtypeStruct(cot.shape, bf16),
            jax.ShapeDtypeStruct(proj.shape, bf16),
            jax.ShapeDtypeStruct((n, slab, inner), f32),
        ],
        cost_estimate=cost(2000 * size, 24 * size),
        name="results",
    )(proj, cot, prev, last, after, taps, skip, row_param, conv_pos, corr_pos)
    return (
        layer_out.reshape(1, channels, inner),
        proj_grad.reshape(1, 3, channels, inner),
        filter_grad.reshape(n * slab, inner),
    )


PARTS = 3
WIDTH = 16


def thirds(value):
    high = value.astype(bf16)
    rest = value - high.astype(f32)
    mid = rest.astype(bf16)
    low = (rest - mid.astype(f32)).astype(bf16)
    return [high, mid, low]


def halves(value):
    high = value.astype(bf16)
    return [high, (value - high.astype(f32)).astype(bf16)]


def spread_table(inner, count):
    row = np.arange(PARTS * WIDTH)[:, None] % WIDTH
    col = np.arange(count * inner)[None, :] // inner
    return (row == col).astype(jnp.bfloat16)


def shift_table(inner, step):
    return np.concatenate([np.eye(inner, k=step), np.eye(inner, k=2 * step)], axis=1).astype(jnp.bfloat16)


def spot_table(rows, cols, pairs):
    table = np.zeros((rows, cols), np.float32)
    for a, b in pairs:
        table[a, b] = 1.0
    return table.astype(jnp.bfloat16)


def edge_table(inner):
    return np.stack(
        [
            spot_table(
                16,
                inner,
                ([(2 * m, inner - 2), (2 * m + 1, inner - 1)] if m < 3 else []) + [(8 + 2 * m, 0), (9 + 2 * m, 1)],
            )
            for m in range(4)
        ]
    )


def before_table(inner):
    return np.stack(
        [spot_table(inner, 2 * inner, [(2 * m + 1, 0), (2 * m, inner), (2 * m + 1, inner + 1)]) for m in range(3)]
    )


def after_table(inner):
    spots = []
    for m in range(3):
        for part in (0, 8):
            spots += [(part + 2 * m, inner * (m + 1) - 2), (part + 2 * m + 1, inner * (m + 1) - 1)]
    return spot_table(16, 3 * inner, spots)


def ring(index, shift, count):
    return lax.rem(index + shift + count, count)


def folded(value):
    return jnp.concatenate([value[:, i : i + 128] for i in range(0, value.shape[1], 128)], axis=0)


def unfolded(value, rows):
    count = value.shape[0] // rows
    return jnp.concatenate([value[i * rows : (i + 1) * rows] for i in range(count)], axis=1)


def param_kernel(groups, taps_ref, skip_ref, row_ref, part_ref, line_ref):
    n, _, rows = row_ref.shape
    slab = rows // groups
    line_ref[...] = jnp.zeros(line_ref.shape, f32)
    for m in range(3):
        line_ref[3 * m : 3 * m + 3] = taps_ref[m]
    line_ref[9:10] = skip_ref[...]
    value = line_ref[...]
    for k in range(n):
        pieces = [value[:, (d * n + k) * slab : (d * n + k + 1) * slab] for d in range(groups)]
        mine = jnp.concatenate(pieces, axis=1)
        row_ref[k] = mine
        part_ref[k] = jnp.concatenate(thirds(mine), axis=0)


def send_kernel(n, me_ref, proj_ref, cot_ref, param_ref, spread_ref, shift_ref, pick_ref, *refs):
    outs, (last_ref, first_ref, tap_ref, move_ref, stage_ref) = refs[:n], refs[n:]
    groups, _, slab, inner = cot_ref.shape
    rows = groups * slab
    me = me_ref[0]

    @pl.loop(0, n)
    def _(e):
        k = ring(me, e, n)
        tap_ref[...] = tn(param_ref[k], spread_ref[...])
        edges = jnp.zeros((16, rows), f32)
        for m in range(4):
            block = (proj_ref[m, :, k] if m < 3 else cot_ref[:, k]).reshape(rows, inner)
            edges += nt(pick_ref[m], block)
            if m < 3:
                move_ref[m] = jnp.dot(block, shift_ref[...], preferred_element_type=f32)
        last_ref[k] = edges[:8].astype(bf16)
        first_ref[k] = edges[8:].astype(bf16)
        stage_ref[e, 2 * rows :] = folded(edges).astype(bf16)
        for d in range(groups):
            here = slice(d * slab, (d + 1) * slab)
            taps = [tap_ref[here, j * inner : (j + 1) * inner] for j in range(9)]
            act = []
            for m in range(3):
                x = proj_ref[m, d, k].astype(f32)
                x1, x2 = move_ref[m, here, :inner], move_ref[m, here, inner:]
                act.append(taps[3 * m] * x + taps[3 * m + 1] * x1 + taps[3 * m + 2] * x2)
            stage_ref[e, here] = (act[0] * act[2]).astype(bf16)
            stage_ref[e, rows + d * slab : rows + (d + 1) * slab] = (cot_ref[d, k].astype(f32) * act[1]).astype(bf16)

    for e in range(n):
        outs[e][...] = stage_ref[e]


def act_kernel(n, proj_ref, prev_ref, param_ref, spread_ref, place_ref, shift_ref, before_ref, *refs):
    act_ref, tap_ref, move_ref = refs[-3:]
    _, groups, _, slab, inner = proj_ref.shape
    rows = groups * slab

    @pl.loop(0, n)
    def _(k):
        tap_ref[...] = tn(param_ref[k], spread_ref[...])
        early = tn(prev_ref[k], place_ref[...]).astype(bf16)
        for m in range(3):
            block = proj_ref[m, :, k].reshape(rows, inner)
            both = jnp.concatenate([block, early], axis=1)
            table = jnp.concatenate([shift_ref[...], before_ref[m]], axis=0)
            move_ref[m] = jnp.dot(both, table, preferred_element_type=f32)
        for d in range(groups):
            here = slice(d * slab, (d + 1) * slab)
            taps = [tap_ref[here, j * inner : (j + 1) * inner] for j in range(9)]
            for m in range(3):
                x = proj_ref[m, d, k].astype(f32)
                x1, x2 = move_ref[m, here, :inner], move_ref[m, here, inner:]
                act_ref[m, d, k] = taps[3 * m] * x + taps[3 * m + 1] * x1 + taps[3 * m + 2] * x2


def pair_after(param, late, early, cot):
    results = []
    for t in range(2):
        ahead = []
        for m in range(3):
            now = late[2 * m + t : 2 * m + t + 1]
            one = early[2 * m + 1 : 2 * m + 2] if t == 0 else late[2 * m : 2 * m + 1]
            two = early[2 * m : 2 * m + 1] if t == 0 else early[2 * m + 1 : 2 * m + 2]
            taps = [param[3 * m + j : 3 * m + j + 1] for j in range(3)]
            ahead.append(taps[0] * now + taps[1] * one + taps[2] * two)
        gate = (ahead[0] * ahead[2]).astype(bf16)
        grad = (cot[t : t + 1] * ahead[1]).astype(bf16)
        results.append((ahead, gate.astype(f32), grad.astype(f32)))
    return results


def stacked(rows, parts):
    line = lax.broadcasted_iota(jnp.int32, (8, rows), 0)
    total = jnp.zeros((8, rows), f32)
    for i, part in enumerate(parts):
        total = jnp.where(line == i, part, total)
    return total


def signal_kernel(n, groups, me_ref, row_ref, fix_ref, small_ref, large_ref, *refs):
    got = refs[:n]
    gate_spec, grad_spec, own_ref, *pieces = refs[-groups - 6 : -4]
    edge_ref, gate_ref, grad_ref, part_ref = refs[-4:]
    _, rows, inner = gate_ref.shape
    slab = rows // groups
    me, my_group = me_ref[0], me_ref[1]
    edge_ref[0] = jnp.zeros(edge_ref.shape[1:], f32)
    for e in range(n):
        edge_ref[ring(me, -e, n) + 1] = unfolded(got[e][2 * rows :].astype(f32), 16)
    param = row_ref[me]
    lane = lax.broadcasted_iota(jnp.int32, (rows, inner), 1)
    for e in range(n):
        p = ring(me, -e, n)
        early, late = edge_ref[p], edge_ref[p + 1]
        pair = pair_after(param, late[8:14], early[:8], late[14:16])
        fix = stacked(rows, [pair[0][1], pair[1][1], pair[0][2], pair[1][2]])
        placed = tn(fix.astype(bf16), fix_ref[...])
        gate_ref[p] = jnp.where(lane < 2, placed[:, :inner], got[e][:rows].astype(f32)).astype(bf16)
        grad_ref[p] = jnp.where(lane < 2, placed[:, inner:], got[e][rows : 2 * rows].astype(f32)).astype(bf16)
    spectrum(gate_ref, small_ref, large_ref, gate_spec)
    spectrum(grad_ref, small_ref, large_ref, grad_spec)
    parts = product_inverse(gate_spec, grad_spec, True, small_ref, large_ref, n * inner // 4)
    for k, block in enumerate(blocks_of(parts, inner)):
        part_ref[k] = block
    for k in range(n):
        own_ref[k] = part_ref[k, pl.ds(pl.multiple_of(my_group * slab, slab), slab)]
        for e in range(1, groups):
            at = pl.multiple_of(ring(my_group, e, groups) * slab, slab)
            pieces[e - 1][k] = part_ref[k, pl.ds(at, slab)].astype(bf16)


def filter_kernel(groups, me_ref, small_ref, large_ref, *refs):
    got, (spec_ref, filt_ref) = refs[:groups], refs[groups:]
    n, slab, _ = got[0].shape
    for e in range(groups):
        at = pl.multiple_of(ring(me_ref[1], -e, groups) * slab, slab)
        for k in range(n):
            filt_ref[k, pl.ds(at, slab)] = got[e][k]
    spectrum(filt_ref, small_ref, large_ref, spec_ref)


def store_result(out_ref, blocks, rows, inner):
    rounded = [b.astype(bf16) for b in blocks]
    for k, block in enumerate(rounded):
        out_ref[k, :rows] = block
        if k + 1 < len(rounded):
            tail = nt(pick(8, inner, [(0, 0), (1, 1)]), rounded[k + 1])
        else:
            tail = jnp.zeros((8, rows), f32)
        out_ref[k, rows:] = folded(tail).astype(bf16)


def conv_kernel(n, inner, filt_spec, gate_spec, small_ref, large_ref, out_ref):
    rows = gate_spec.shape[0]
    parts = product_inverse(filt_spec, gate_spec, False, small_ref, large_ref, n * inner // 4)
    store_result(out_ref, blocks_of(parts, inner), rows, inner)


def corr_kernel(n, groups, me_ref, filt_spec, grad_spec, small_ref, large_ref, conv_ref, own_ref, *refs):
    got, outs, corr_ref = refs[: groups - 1], refs[groups - 1 : groups - 1 + n], refs[-1]
    rows = grad_spec.shape[0]
    height, inner = corr_ref.shape[1:]
    parts = product_inverse(filt_spec, grad_spec, True, small_ref, large_ref, n * inner // 4)
    store_result(corr_ref, blocks_of(parts, inner), rows, inner)
    for e in range(n):
        k = ring(me_ref[0], e, n)
        outs[e][:height] = conv_ref[k]
        outs[e][height : 2 * height] = corr_ref[k]
        total = own_ref[k]
        for other in got:
            total = total + other[k].astype(f32)
        outs[e][2 * height :] = total.astype(bf16)


def final_kernel(
    n, scale, me_ref, act_ref, cot_ref, last_ref, next_ref, param_ref, row_ref, spread_ref, shift_ref, after_ref, *refs
):
    got = refs[:n]
    out_ref, pg_ref, fg_ref, tap_ref, late_ref, move_ref, grad_ref, stage_ref = refs[n:]
    groups, _, slab, inner = cot_ref.shape
    rows = groups * slab
    height = rows + rows // 16
    for e in range(n):
        stage_ref[e] = got[e][...]

    @pl.loop(0, n)
    def _(e):
        k = ring(me_ref[0], -e, n)
        fg_ref[k] = stage_ref[e, 2 * height :].astype(f32) * scale
        tap_ref[...] = tn(param_ref[k], spread_ref[...])
        conv_tail = unfolded(stage_ref[e, rows:height].astype(f32), 8)
        corr_tail = unfolded(stage_ref[e, height + rows : 2 * height].astype(f32), 8)
        param = row_ref[k]
        keep = param[9:10]
        own, late = last_ref[k].astype(f32), next_ref[k].astype(f32)
        spare = []
        for t, (ahead, gate_t, grad_t) in enumerate(pair_after(param, late[:6], own, late[6:8])):
            mixed_t = conv_tail[t : t + 1] + keep * gate_t
            gate_grad_t = corr_tail[t : t + 1] + keep * grad_t
            spare.append((gate_grad_t * ahead[2], late[6 + t : 7 + t] * mixed_t, gate_grad_t * ahead[0]))
        ends = []
        for m in range(3):
            one, two = param[3 * m + 1 : 3 * m + 2], param[3 * m + 2 : 3 * m + 3]
            ends += [two * spare[0][m], one * spare[0][m] + two * spare[1][m]]
        late_ref[...] = tn(jnp.concatenate(halves(stacked(rows, ends)), axis=0), after_ref[...])
        for d in range(groups):
            here = slice(d * slab, (d + 1) * slab)
            skip = tap_ref[here, 9 * inner : 10 * inner]
            first, second, value = act_ref[0, d, k], act_ref[1, d, k], act_ref[2, d, k]
            upstream = cot_ref[d, k].astype(f32)
            gate = (first * value).astype(bf16).astype(f32)
            grad = (upstream * second).astype(bf16).astype(f32)
            mixed = stage_ref[e, here].astype(f32) + skip * gate
            out_ref[d, k] = (second * mixed).astype(bf16)
            gate_grad = stage_ref[e, height + d * slab : height + (d + 1) * slab].astype(f32) + skip * grad
            for m, x in enumerate((gate_grad * value, upstream * mixed, gate_grad * first)):
                high, low = halves(x)
                move_ref[m, here, :inner] = high
                move_ref[m, here, inner:] = low
                grad_ref[m, here] = x
        for m in range(3):
            moved = jnp.dot(
                move_ref[m], jnp.concatenate([shift_ref[...]] * 2, axis=0), preferred_element_type=f32
            )
            taps = [tap_ref[:, j * inner : (j + 1) * inner] for j in range(3 * m, 3 * m + 3)]
            back = taps[0] * grad_ref[m] + taps[1] * moved[:, :inner] + taps[2] * moved[:, inner:]
            back = (back + late_ref[:, inner * m : inner * (m + 1)]).astype(bf16)
            for d in range(groups):
                pg_ref[m, d, k] = back[d * slab : (d + 1) * slab]


def peer_shards(projections, short_filter, long_filter, skip_gain, cotangent):
    groups = lax.axis_size("dp")
    n = lax.axis_size("ctx")
    channels = projections.shape[2]
    inner = projections.shape[3]
    slab = channels // (groups * n)
    rows = groups * slab
    length = inner * n
    q = length // 4
    scale = 1.0 / math.sqrt(groups * length)
    size = channels * inner

    place = jnp.stack([lax.axis_index("ctx"), lax.axis_index("dp")]).astype(jnp.int32)
    proj = projections.reshape(3, groups, n, slab, inner)
    cot = cotangent.reshape(groups, n, slab, inner)
    filt = long_filter.reshape(groups, n, slab, inner)
    small, large = (jnp.asarray(t) for t in dft_tables(q))

    def call(kernel, outs, work, args, scratch=(), limit=24):
        moved = sum(math.prod(a.shape) * a.dtype.itemsize for a in [*args, *outs])

        def full(a):
            if a is small or a is large or (a.dtype == f32 and math.prod(a.shape) >= rows * 8 * q):
                return pl.BlockSpec(memory_space=pltpu.VMEM)
            return pl.BlockSpec(a.shape, lambda i, *_: (0,) * len(a.shape))

        scalars = 1 if args[0] is place else 0
        return pl.pallas_call(
            kernel,
            grid_spec=pltpu.PrefetchScalarGridSpec(
                num_scalar_prefetch=scalars,
                grid=(1,),
                in_specs=[full(a) for a in args[scalars:]],
                out_specs=[full(a) for a in outs],
                scratch_shapes=list(scratch),
            ),
            out_shape=outs,
            cost_estimate=cost(work, moved),
            compiler_params=pltpu.CompilerParams(vmem_limit_bytes=limit * 2**20),
        )(*args)

    def array(*shape, dtype=bf16):
        return jax.ShapeDtypeStruct(shape, dtype)

    def to_peers(messages, axis):
        count = lax.axis_size(axis)
        got = []
        for e, message in enumerate(messages, 1):
            got.append(lax.ppermute(message, axis, [(i, (i + e) % count) for i in range(count)]))
        return got

    row_param, param = call(
        functools.partial(param_kernel, groups),
        [array(n, WIDTH, rows, dtype=f32), array(n, PARTS * WIDTH, rows)],
        channels * 200,
        [jnp.transpose(short_filter, (0, 2, 1)), skip_gain.reshape(1, channels)],
        [pltpu.VMEM((WIDTH, channels), f32)],
    )
    mine = lax.dynamic_index_in_dim(filt, place[1], 0, keepdims=False).astype(bf16)
    quarter = lax.all_to_all(mine, "ctx", split_axis=0, concat_axis=0, tiled=True)
    spread9, spread10 = jnp.asarray(spread_table(inner, 9)), jnp.asarray(spread_table(inner, 10))
    delay, advance = jnp.asarray(shift_table(inner, 1)), jnp.asarray(shift_table(inner, -1))
    message = array(2 * rows + rows // 8, inner)
    *sent, last, first = call(
        functools.partial(send_kernel, n),
        [message] * n + [array(n, 8, rows)] * 2,
        2000 * size,
        [place, proj, cot, param, spread9, delay, jnp.asarray(edge_table(inner))],
        [
            pltpu.VMEM((rows, 9 * inner), f32),
            pltpu.VMEM((3, rows, 2 * inner), f32),
            pltpu.VMEM((n, *message.shape), bf16),
        ],
        limit=60,
    )
    got = [sent[0], *to_peers(sent[1:], "ctx")]
    forth = [(i, i + 1) for i in range(n - 1)]
    prev = lax.ppermute(last, "ctx", forth)
    after = lax.ppermute(first, "ctx", [(b, a) for a, b in forth])
    shared = [quarter, *to_peers([quarter] * (groups - 1), "dp")]

    dft = 2 * rows * 14 * q * q
    spec = array(rows, 8 * q, dtype=f32)
    (filt_spec,) = call(
        functools.partial(filter_kernel, groups),
        [spec],
        2 * dft,
        [place, small, large, *shared],
        [pltpu.VMEM((n, rows, inner), bf16)],
    )
    fix = jnp.asarray(spot_table(8, 2 * inner, [(0, 0), (1, 1), (2, inner), (3, inner + 1)]))
    gate_spec, grad_spec, own, *pieces = call(
        functools.partial(signal_kernel, n, groups),
        [spec, spec, array(n, slab, inner, dtype=f32)] + [array(n, slab, inner)] * (groups - 1),
        5 * dft,
        [place, row_param, fix, small, large, *got, prev, after, filt_spec],
        [
            pltpu.VMEM((n + 1, 16, rows), f32),
            pltpu.VMEM((n, rows, inner), bf16),
            pltpu.VMEM((n, rows, inner), bf16),
            pltpu.VMEM((n, rows, inner), f32),
        ],
    )
    others = to_peers(pieces, "dp")
    height = rows + rows // 16
    (conv,) = call(
        functools.partial(conv_kernel, n, inner), [array(n, height, inner)], dft, [filt_spec, gate_spec, small, large]
    )
    back = array(2 * height + slab, inner)
    sent = call(
        functools.partial(corr_kernel, n, groups),
        [back] * n,
        dft,
        [place, filt_spec, grad_spec, small, large, conv, own, *others],
        [pltpu.VMEM((n, height, inner), bf16)],
    )
    got = [sent[0], *to_peers(sent[1:], "ctx")]
    (act,) = call(
        functools.partial(act_kernel, n),
        [array(*proj.shape, dtype=f32)],
        1000 * size,
        [
            proj, prev, param, spread9, jnp.asarray(spot_table(8, inner, [(i, i) for i in range(6)])), delay,
            jnp.asarray(before_table(inner)), sent[0],
        ],
        [pltpu.VMEM((rows, 9 * inner), f32), pltpu.VMEM((3, rows, 2 * inner), f32)],
    )
    layer_out, proj_grad, filter_grad = call(
        functools.partial(final_kernel, n, scale),
        [array(*cot.shape), array(*proj.shape), array(n, slab, inner, dtype=f32)],
        2000 * size,
        [
            place, act, cot, last, after, param, row_param, spread10, advance, jnp.asarray(after_table(inner)), *got
        ],
        [
            pltpu.VMEM((rows, 10 * inner), f32),
            pltpu.VMEM((rows, 3 * inner), f32),
            pltpu.VMEM((3, rows, 2 * inner), bf16),
            pltpu.VMEM((3, rows, inner), f32),
            pltpu.VMEM((n, *back.shape), bf16),
        ],
    )
    return (
        layer_out.reshape(1, channels, inner),
        proj_grad.reshape(1, 3, channels, inner),
        filter_grad.reshape(n * slab, inner),
    )


def fits(mesh_sizes, channels, inner):
    n = mesh_sizes["ctx"]
    q = inner * n // 4
    return n % 4 == 0 and (channels // n) % 128 == 0 and 2 * (14 * q * q) <= TABLE_BYTES


def shards(projections, short_filter, long_filter, skip_gain, cotangent):
    sizes = {axis: lax.axis_size(axis) for axis in ("dp", "ctx")}
    if not fits(sizes, projections.shape[2], projections.shape[3]):
        return wide_shards(projections, short_filter, long_filter, skip_gain, cotangent)
    return peer_shards(projections, short_filter, long_filter, skip_gain, cotangent)


def solution(mesh):
    placed = (P("dp", None, None, "ctx"), P(), P(None, "ctx"), P(), P("dp", None, "ctx"))
    return jax.shard_map(
        shards,
        mesh=mesh,
        in_specs=placed,
        out_specs=(P("dp", None, "ctx"), P("dp", None, None, "ctx"), P("dp", "ctx")),
        check_vma=False,
    )
```
